32 devices in a mesh: blk: 8 (over z, x), rep: 4 (over y, core).
Axes of the slice: x: 2, y: 2, z: 4, core: 2. Of those that a mesh axis runs over, the one named last changes fastest.
Arguments:
- points: bfloat16 [6144, 1024], P('blk'), may hold values from -6 to 6
- w_in: bfloat16 [1024, 512], replicated, may hold values from -0.1875 to 0.1875
- b_in: float32 [512], replicated, may hold values from -3 to 3
- w_out: bfloat16 [512, 64], replicated, may hold values from -0.25 to 0.25
- inv_scale: float32 [64], replicated, may hold values from 0.05 to 0.5
- solves: bfloat16 [64, 6144], P(None, 'blk'), may hold values from -1.6875 to 1.6875
- probes: bfloat16 [64, 6144], P(None, 'blk'), may hold values from -1.6875 to 1.6875
Outputs:
- feat_grad: float32 [64, 6144], P(None, ('blk', 'rep'))
- grad_w_in: float32 [1024, 512], replicated
- grad_b_in: float32 [512], replicated
- grad_w_out: float32 [512, 64], replicated
The draws below stay inside these ranges and needn't reach their ends.
All inputs are finite; a program needn't handle non-finite values.
Results may differ from the reference program's by a relative error of at most 0.034.
Values may be sent and summed in bfloat16 or wider, within the bound.
No kernel may reach another device: no remote copies, remote signals or barrier semaphores. Data moves between devices by JAX's collectives and lax.ppermute only.
A program may use at most 64 MiB of HBM per device.

```python
import math
import jax
import jax.numpy as jnp
from jax import lax

DIN = 1024
HID = 512
FEAT = 64
PAIRS = 64
TOK_DEV = 768
NPTS = 6144
N_REP = 4


def block_scale(rng, dims, shards, least, largest):
    def one(axis_at, shards_of):
        steps = jax.random.uniform(jax.random.fold_in(jax.random.fold_in(rng, 6), axis_at), (shards_of,), jnp.float32, least / len(shards), largest / len(shards))
        return jnp.repeat(jnp.exp(steps), dims[axis_at] // shards_of).reshape((-1,) + (1,) * (len(dims) - axis_at - 1))

    loudness = one(*shards[0])
    for cut in shards[1:]:
        loudness = loudness * one(*cut)
    return loudness


def normal_values(stream_key, shape, deviation, limit, shards=(), dtype=jnp.bfloat16):
    level = block_scale(stream_key, shape, shards, -0.22, 0.18) if shards else 1.0
    array = jax.random.normal(stream_key, shape, jnp.float32) * deviation * level
    return jnp.minimum(jnp.maximum(array, -limit), limit).astype(dtype)


def setup_inputs(seed: int = 0) -> dict:
    key_of = jax.random.split(jax.random.key(seed), 8)
    points = normal_values(key_of[0], (NPTS, DIN), 1.0, 6.0, ((0, 8),))
    w_in = normal_values(key_of[1], (DIN, HID), DIN ** -0.5, 0.1875)
    b_in = normal_values(key_of[2], (HID,), 0.5, 3.0, (), jnp.float32)
    w_out = normal_values(key_of[3], (HID, FEAT), HID ** -0.5, 0.25)
    inv_scale = jnp.clip(jnp.exp(jax.random.uniform(key_of[4], (FEAT,), jnp.float32, math.log(0.05), math.log(0.5))), 0.05, 0.5)
    solves = normal_values(key_of[5], (PAIRS, NPTS), (2.5 / NPTS ** 0.25), 1.6875, ((1, 8),))
    probes = normal_values(key_of[6], (PAIRS, NPTS), (2.5 / NPTS ** 0.25), 1.6875, ((1, 8),))
    return {"points": points, "w_in": w_in, "b_in": b_in, "w_out": w_out, "inv_scale": inv_scale, "solves": solves, "probes": probes}


def couple(own_y, own_pair, own_sq, visitor, feat):
    vis_y = visitor[:feat]
    vis_pair = visitor[feat:]
    vis_sq = lax.optimization_barrier(jnp.sum(jnp.square(vis_y.astype(jnp.float32)), axis=0))
    cross = lax.dot_general(own_y, vis_y, (((0,), (0,)), ((), ())), preferred_element_type=jnp.float32)
    kernel = jnp.exp(-0.5 * (own_sq[:, None] + vis_sq[None, :] - 2.0 * cross))
    coupling = lax.dot_general(own_pair, vis_pair, (((0,), (0,)), ((), ())), preferred_element_type=jnp.float32)
    weight_b = (coupling * kernel).astype(jnp.bfloat16)
    totals = lax.optimization_barrier(jnp.sum(weight_b.astype(jnp.float32), axis=1))
    pull = lax.dot_general(vis_y, weight_b, (((1,), (1,)), ((), ())), preferred_element_type=jnp.float32)
    return (totals, pull)

def reference(points, w_in, b_in, w_out, inv_scale, solves, probes):
    hidden = jnp.tanh(jnp.dot(points, w_in, preferred_element_type=jnp.float32) + b_in).astype(jnp.bfloat16)
    pre = lax.dot_general(w_out, hidden, (((0,), (1,)), ((), ())), preferred_element_type=jnp.float32)
    scaled = (pre * inv_scale[:, None]).astype(jnp.bfloat16)
    sq = lax.optimization_barrier(jnp.sum(jnp.square(scaled.astype(jnp.float32)), axis=0))
    own_pair = jnp.concatenate([solves, probes], axis=0)
    visitor = jnp.concatenate([scaled, probes, solves], axis=0)
    blocks = NPTS // TOK_DEV
    width = TOK_DEV * N_REP
    cols = NPTS // width
    rows_y = scaled.reshape(FEAT, blocks, TOK_DEV).transpose(1, 0, 2)
    rows_pair = own_pair.reshape(2 * PAIRS, blocks, TOK_DEV).transpose(1, 0, 2)
    rows_sq = sq.reshape(blocks, TOK_DEV)
    col_vis = visitor.reshape(FEAT + 2 * PAIRS, cols, width).transpose(1, 0, 2)

    def one_row(item):
        own_y, pair_rows, sq_rows = item

        def step(carry, vis):
            totals, pull = couple(own_y, pair_rows, sq_rows, vis, FEAT)
            return ((carry[0] + totals, carry[1] + pull), None)
        init = (jnp.zeros((TOK_DEV,), jnp.float32), jnp.zeros((FEAT, TOK_DEV), jnp.float32))
        result, unused = lax.scan(step, init, col_vis)
        return result
    totals, pull = lax.map(one_row, (rows_y, rows_pair, rows_sq))
    totals = totals.reshape(NPTS)
    pull = pull.transpose(1, 0, 2).reshape(FEAT, NPTS)
    feat_grad = (pull - scaled.astype(jnp.float32) * totals[None, :]) * inv_scale[:, None]
    grad_b16 = feat_grad.astype(jnp.bfloat16)
    back = lax.dot_general(grad_b16, w_out, (((0,), (1,)), ((), ())), preferred_element_type=jnp.float32)
    hid32 = hidden.astype(jnp.float32)
    pre_grad = back * (1.0 - hid32 * hid32)
    norm = 1.0 / jnp.sqrt(jnp.float32(NPTS))
    grad_w_in = lax.dot_general(points, pre_grad.astype(jnp.bfloat16), (((0,), (0,)), ((), ())), preferred_element_type=jnp.float32) * norm
    grad_b_in = lax.optimization_barrier(jnp.sum(pre_grad, axis=0)) * norm
    grad_w_out = lax.dot_general(hidden, grad_b16, (((0,), (1,)), ((), ())), preferred_element_type=jnp.float32) * norm
    return (feat_grad, grad_w_in, grad_b_in, grad_w_out)
```

```python
import math

import jax
import jax.numpy as jnp
from jax import lax
from jax.sharding import PartitionSpec as P

AXES = ("blk", "rep")
BF16 = jnp.bfloat16
F32 = jnp.float32


def bits_of(count):
    return count.bit_length() - 1


def visit_mask(step, rep, blocks, reps):
    low = (bits_of(reps) + 1) // 2
    high = bits_of(reps) - low
    near, far = divmod(rep, 1 << high)
    return far * (blocks >> high) + step * (1 << low) + near


def fetch(array, masks, blocks, reps):
    route = [((b ^ masks[r]) * reps + r, b * reps + r) for b in range(blocks) for r in range(reps)]
    return lax.ppermute(array, AXES, route)


def swap(array, blk_mask, rep_mask, blocks, reps):
    route = [
        (b * reps + r, (b ^ blk_mask) * reps + (r ^ rep_mask))
        for b in range(blocks)
        for r in range(reps)
    ]
    return lax.ppermute(array, AXES, route)


def couple(own_y, own_pair, own_sq, visitor, feat):
    vis_y = visitor[:feat]
    vis_pair = visitor[feat:]
    vis_sq = jnp.sum(jnp.square(vis_y.astype(F32)), axis=0)
    cross = lax.dot_general(own_y, vis_y, (((0,), (0,)), ((), ())), preferred_element_type=F32)
    kernel = jnp.exp(-0.5 * (own_sq[:, None] + vis_sq[None, :] - 2.0 * cross))
    coupling = lax.dot_general(
        own_pair, vis_pair, (((0,), (0,)), ((), ())), preferred_element_type=F32
    )
    weight_b = (coupling * kernel).astype(BF16)
    totals = jnp.sum(weight_b.astype(F32), axis=1)
    pull = lax.dot_general(vis_y, weight_b, (((1,), (1,)), ((), ())), preferred_element_type=F32)
    return (totals, pull)


def on_device(points, w_in, b_in, w_out, inv_scale, solves, probes):
    feat = w_out.shape[1]
    reps = lax.axis_size("rep")
    blocks = lax.axis_size("blk")
    rep_index = lax.axis_index("rep")
    blk_index = lax.axis_index("blk")
    rows, din = points.shape
    hid = w_in.shape[1]
    npts = rows * blocks
    quarter = rows // reps
    cols = hid // reps

    hidden = jnp.tanh(jnp.dot(points, w_in, preferred_element_type=F32) + b_in).astype(BF16)
    pre = lax.dot_general(w_out, hidden, (((0,), (1,)), ((), ())), preferred_element_type=F32)
    scaled = (pre * inv_scale[:, None]).astype(BF16)
    own_sq = jnp.sum(jnp.square(scaled.astype(F32)), axis=0)
    own_pair = jnp.concatenate([solves, probes], axis=0)
    visitor = jnp.concatenate([scaled, probes, solves], axis=0)

    visitors = []
    for step in range(blocks // reps):
        masks = [visit_mask(step, r, blocks, reps) for r in range(reps)]
        visitors.append(fetch(visitor, masks, blocks, reps))
    totals = jnp.zeros((rows,), F32)
    pull = jnp.zeros((feat, rows), F32)
    for vis in visitors:
        more_totals, more_pull = couple(scaled, own_pair, own_sq, vis, feat)
        totals = totals + more_totals
        pull = pull + more_pull
    drift = pull - scaled.astype(F32) * totals[None, :]

    drift = drift + swap(drift, 0, 1, blocks, reps)
    for bit in range(1, bits_of(reps)):
        sent = drift.astype(BF16)
        got = swap(sent, 0, 1 << bit, blocks, reps)
        drift = sent.astype(F32) + got.astype(F32)
    full_grad = drift * inv_scale[:, None]
    feat_grad = lax.dynamic_slice_in_dim(full_grad, rep_index * quarter, quarter, 1)
    grad_b16 = full_grad.astype(BF16)

    first = rep_index * cols
    own_hidden = lax.dynamic_slice_in_dim(hidden, first, cols, 1)
    own_w_out = lax.dynamic_slice_in_dim(w_out, first, cols, 0)
    back = lax.dot_general(
        grad_b16, own_w_out, (((0,), (1,)), ((), ())), preferred_element_type=F32
    )
    hid32 = own_hidden.astype(F32)
    pre_grad = back * (1.0 - hid32 * hid32)
    norm = 1.0 / math.sqrt(npts)
    term_w_in = lax.dot_general(
        points, pre_grad.astype(BF16), (((0,), (0,)), ((), ())), preferred_element_type=F32
    )
    term_b_in = jnp.sum(pre_grad, axis=0)
    term_w_out = lax.dot_general(
        grad_b16, own_hidden, (((1,), (0,)), ((), ())), preferred_element_type=F32
    )
    bias = jnp.broadcast_to(term_b_in[None, None], (2, 16, cols))
    halves = jnp.concatenate(
        [term_w_in.reshape(2, din // 2, cols), term_w_out.reshape(2, feat // 2, cols), bias], axis=1
    )
    halves = (halves * norm).astype(BF16)

    side = blk_index % 2
    kept = lax.dynamic_index_in_dim(halves, side, 0, keepdims=False)
    sent = lax.dynamic_index_in_dim(halves, 1 - side, 0, keepdims=False)
    got = swap(sent, 1, 0, blocks, reps)
    part = (kept.astype(F32) + got.astype(F32)).astype(BF16)
    for bit in range(1, bits_of(blocks)):
        got = swap(part, (2 << bit) - 2, 0, blocks, reps)
        part = (part.astype(F32) + got.astype(F32)).astype(BF16)

    masks = [(h, r << 1) for r in range(reps // 2) for h in range(2)]
    pieces = [part] + [swap(part, h, r, blocks, reps) for h, r in masks[1:]]
    near = jnp.stack(pieces)
    other = swap(near, 0, 1, blocks, reps)
    table = jnp.stack([near, other])
    table = table.reshape(2, reps // 2, 2, *part.shape)

    def piece(half, rep):
        index = (
            (rep ^ rep_index) & 1,
            (rep ^ rep_index) >> 1,
            half ^ side,
            0,
            0,
        )
        return lax.dynamic_slice(table, index, (1, 1, 1, *part.shape)).reshape(part.shape)

    whole = jnp.concatenate(
        [jnp.concatenate([piece(h, r) for r in range(reps)], axis=1)[None] for h in range(2)]
    ).astype(F32)
    grad_w_in = whole[:, : din // 2].reshape(din, hid)
    grad_w_out = whole[:, din // 2 : din // 2 + feat // 2].reshape(feat, hid).T
    grad_b_in = whole[0, din // 2 + feat // 2]
    return (feat_grad, grad_w_in, grad_b_in, grad_w_out)


def solution(mesh):
    in_specs = (P("blk", None), P(), P(), P(), P(), P(None, "blk"), P(None, "blk"))
    out_specs = (P(None, ("blk", "rep")), P(), P(), P())
    return jax.shard_map(
        on_device, mesh=mesh, in_specs=in_specs, out_specs=out_specs, check_vma=False
    )
```

```python
import math

import jax
import jax.numpy as jnp
from jax import lax
from jax.experimental import pallas as pl
from jax.experimental.pallas import tpu as pltpu
from jax.sharding import PartitionSpec as P

AXES = ("blk", "rep")
BF16 = jnp.bfloat16
F32 = jnp.float32


def bits_of(count):
    return count.bit_length() - 1


def visit_mask(step, rep, reps):
    width = bits_of(reps)
    core = rep & 1
    near = (core << (width - 1)) | (rep >> 1)
    if width > 1:
        near ^= core ^ (step & 1)
    return step * reps + near


def fetch(array, masks, blocks, reps):
    route = [((b ^ masks[r]) * reps + r, b * reps + r) for b in range(blocks) for r in range(reps)]
    return lax.ppermute(array, AXES, route)


def swap(array, blk_mask, rep_mask, blocks, reps):
    route = [
        (b * reps + r, (b ^ blk_mask) * reps + (r ^ rep_mask))
        for b in range(blocks)
        for r in range(reps)
    ]
    return lax.ppermute(array, AXES, route)


def couple_kernel(chunk, own_y, own_pair, vis_y, vis_pair, before, after):
    feat, rows = own_y.shape
    own = own_y[...]
    own32 = own.astype(F32)
    own_half = 0.5 * jnp.sum(own32 * own32, axis=0, keepdims=True)
    ones = jnp.ones((16, chunk), BF16)
    pulled = jnp.zeros((feat + 16, rows), F32)
    for start in range(0, rows, chunk):
        part_y = vis_y[:, start : start + chunk]
        turned = part_y.astype(F32).T
        vis_half = 0.5 * jnp.sum(turned * turned, axis=1, keepdims=True)
        cross = jnp.dot(turned.astype(BF16), own, preferred_element_type=F32)
        coupling = lax.dot_general(
            vis_pair[:, start : start + chunk],
            own_pair[...],
            (((0,), (0,)), ((), ())),
            preferred_element_type=F32,
        )
        weight = (coupling * jnp.exp(cross - (own_half + vis_half))).astype(BF16)
        pulled += jnp.dot(
            jnp.concatenate([part_y, ones], axis=0), weight, preferred_element_type=F32
        )
    after[...] = before[...] + (pulled[:feat] - own32 * pulled[feat : feat + 1])


def in_vmem(array):
    return pltpu.with_memory_space_constraint(array, pltpu.VMEM)


def couple(own_y, own_pair, vis_y, vis_pair, drift):
    rows = own_y.shape[1]
    chunk = 256 if rows % 256 == 0 else rows
    return pl.pallas_call(
        lambda *refs: couple_kernel(chunk, *refs),
        out_shape=pltpu.VMEM(drift.shape, F32),
        in_specs=[pl.BlockSpec(memory_space=pltpu.VMEM)] * 5,
        out_specs=pl.BlockSpec(memory_space=pltpu.VMEM),
        compiler_params=pltpu.CompilerParams(vmem_limit_bytes=16 << 20),
        name="couple",
    )(*map(in_vmem, (own_y, own_pair, vis_y, vis_pair, drift)))


def place_kernel(depth, offset, where, table, *refs):
    w_in, b_in, w_out = refs[-3:]
    din = w_in.shape[0]
    half = din // 2
    base = 2 * (pl.program_id(0) ^ where[0])
    low = table.at[base + where[1]]
    high = table.at[base + (1 - where[1])]
    w_in[:half] = low[:half].astype(F32)
    w_in[half:] = high[:half].astype(F32)
    turned = jnp.concatenate(
        [low[half : half + depth].astype(F32), high[half : half + depth].astype(F32)], axis=0
    )
    w_out[...] = turned.T
    b_in[...] = low[half + depth : half + depth + 16].astype(F32)[:1]


def place(table, where, offset, din, feat, reps, earlier):
    count, height, cols = table.shape
    hid = cols * reps
    shapes = (
        jax.ShapeDtypeStruct((din, hid), F32),
        jax.ShapeDtypeStruct((1, hid), F32),
        jax.ShapeDtypeStruct((hid, feat), F32),
    )

    def column(i, at):
        return 2 * i + (at[2] ^ offset)

    grid_spec = pltpu.PrefetchScalarGridSpec(
        num_scalar_prefetch=1,
        grid=(reps // 2,),
        in_specs=[pl.BlockSpec(memory_space=pltpu.VMEM)]
        + [pl.BlockSpec(memory_space=pl.ANY) for _ in earlier],
        out_specs=[
            pl.BlockSpec((din, cols), lambda i, at: (0, column(i, at))),
            pl.BlockSpec((1, cols), lambda i, at: (0, column(i, at))),
            pl.BlockSpec((cols, feat), lambda i, at: (column(i, at), 0)),
        ],
    )
    return pl.pallas_call(
        lambda *refs: place_kernel(feat // 2, offset, *refs),
        out_shape=shapes,
        grid_spec=grid_spec,
        input_output_aliases={2 + i: i for i in range(len(earlier))},
        compiler_params=pltpu.CompilerParams(vmem_limit_bytes=16 << 20),
        name="place",
    )(where, in_vmem(table), *earlier)


def on_device(points, w_in, b_in, w_out, inv_scale, solves, probes):
    feat = w_out.shape[1]
    reps = lax.axis_size("rep")
    blocks = lax.axis_size("blk")
    rep_index = lax.axis_index("rep")
    blk_index = lax.axis_index("blk")
    rows, din = points.shape
    hid = w_in.shape[1]
    npts = rows * blocks
    quarter = rows // reps
    cols = hid // reps

    hidden = jnp.tanh(jnp.dot(points, w_in, preferred_element_type=F32) + b_in).astype(BF16)
    pre = lax.dot_general(w_out, hidden, (((0,), (1,)), ((), ())), preferred_element_type=F32)
    scaled = (pre * inv_scale[:, None]).astype(BF16)
    own_pair = jnp.concatenate([solves, probes], axis=0)
    pair = jnp.concatenate([probes, solves], axis=0)
    steps = range(blocks // reps)
    masks = [[visit_mask(step, r, reps) for r in range(reps)] for step in steps]
    pairs = [fetch(pair, masks[step], blocks, reps) for step in steps]
    scaleds = [fetch(scaled, masks[step], blocks, reps) for step in steps]
    drift = jnp.zeros((feat, rows), F32)
    for step in steps:
        drift = couple(scaled, own_pair, scaleds[step], pairs[step], drift)

    drift = drift + swap(drift, 0, 1, blocks, reps)
    for bit in range(1, bits_of(reps)):
        sent = drift.astype(BF16)
        got = swap(sent, 0, 1 << bit, blocks, reps)
        drift = sent.astype(F32) + got.astype(F32)
    full_grad = drift * inv_scale[:, None]
    feat_grad = lax.dynamic_slice_in_dim(full_grad, rep_index * quarter, quarter, 1)
    grad_b16 = full_grad.astype(BF16)

    first = rep_index * cols
    own_hidden = lax.dynamic_slice_in_dim(hidden, first, cols, 1)
    own_w_out = lax.dynamic_slice_in_dim(w_out, first, cols, 0)
    back = lax.dot_general(
        grad_b16, own_w_out, (((0,), (1,)), ((), ())), preferred_element_type=F32
    )
    hid32 = own_hidden.astype(F32)
    pre_grad = back * (1.0 - hid32 * hid32)
    norm = 1.0 / math.sqrt(npts)
    term_w_in = lax.dot_general(
        points, pre_grad.astype(BF16), (((0,), (0,)), ((), ())), preferred_element_type=F32
    )
    term_b_in = jnp.sum(pre_grad, axis=0)
    term_w_out = lax.dot_general(
        grad_b16, own_hidden, (((1,), (0,)), ((), ())), preferred_element_type=F32
    )
    bias = jnp.broadcast_to(term_b_in[None, None], (2, 16, cols))
    halves = jnp.concatenate(
        [term_w_in.reshape(2, din // 2, cols), term_w_out.reshape(2, feat // 2, cols), bias], axis=1
    )
    halves = (halves * norm).astype(BF16)

    side = blk_index % 2
    kept = lax.dynamic_index_in_dim(halves, side, 0, keepdims=False)
    sent = lax.dynamic_index_in_dim(halves, 1 - side, 0, keepdims=False)
    got = swap(sent, 1, 0, blocks, reps)
    part = (kept.astype(F32) + got.astype(F32)).astype(BF16)
    for bit in range(1, bits_of(blocks)):
        got = swap(part, (2 << bit) - 2, 0, blocks, reps)
        part = (part.astype(F32) + got.astype(F32)).astype(BF16)

    masks = [(h, r << 1) for r in range(reps // 2) for h in range(2)]
    pieces = [part] + [swap(part, h, r, blocks, reps) for h, r in masks[1:]]
    near = jnp.stack(pieces)
    other = swap(near, 0, 1, blocks, reps)
    where = jnp.stack([rep_index >> 1, side, rep_index & 1])
    outs = place(near, where, 0, din, feat, reps, ())
    grad_w_in, grad_b_in, grad_w_out = place(other, where, 1, din, feat, reps, outs)
    grad_b_in = grad_b_in.reshape(hid)
    return (feat_grad, grad_w_in, grad_b_in, grad_w_out)


def solution(mesh):
    in_specs = (P("blk", None), P(), P(), P(), P(), P(None, "blk"), P(None, "blk"))
    out_specs = (P(None, ("blk", "rep")), P(), P(), P())
    return jax.shard_map(
        on_device, mesh=mesh, in_specs=in_specs, out_specs=out_specs, check_vma=False
    )
```

```python
import math

import jax
import jax.numpy as jnp
from jax import lax
from jax.experimental import pallas as pl
from jax.experimental.pallas import tpu as pltpu
from jax.sharding import PartitionSpec as P


AXES = ("blk", "rep")
BF16 = jnp.bfloat16
F32 = jnp.float32


def bits_of(count):
    return count.bit_length() - 1


def visit_mask(step, rep, reps):
    width = bits_of(reps)
    core = rep & 1
    near = (core << (width - 1)) | (rep >> 1)
    if width > 1:
        near ^= core ^ (step & 1)
    return step * reps + near


def fetch(array, masks, blocks, reps):
    route = [((b ^ masks[r]) * reps + r, b * reps + r) for b in range(blocks) for r in range(reps)]
    return lax.ppermute(array, AXES, route)


def swap(array, blk_masks, rep_mask, blocks, reps):
    route = [
        (b * reps + r, (b ^ blk_masks[r & 1]) * reps + (r ^ rep_mask))
        for b in range(blocks)
        for r in range(reps)
    ]
    return lax.ppermute(array, AXES, route)


def join_kernel(first, second, joined, sems):
    count = first.shape[0]
    copies = [
        pltpu.make_async_copy(first, joined.at[:count], sems.at[0]),
        pltpu.make_async_copy(second, joined.at[count:], sems.at[1]),
    ]
    for copy in copies:
        copy.start()
    for copy in copies:
        copy.wait()


def join(first, second):
    count, rows = first.shape
    return pl.pallas_call(
        join_kernel,
        out_shape=pltpu.VMEM((2 * count, rows), first.dtype),
        in_specs=[pl.BlockSpec(memory_space=pl.ANY)] * 2,
        out_specs=pl.BlockSpec(memory_space=pltpu.VMEM),
        scratch_shapes=[pltpu.SemaphoreType.DMA((2,))],
        name="join",
    )(first, second)


def couple_kernel(chunk, own_y, own_pair, vis_y, vis_pair, before, after):
    feat, rows = own_y.shape
    count = own_pair.shape[0] // 2
    crossed = jnp.concatenate([own_pair[count:], own_pair[:count]], axis=0)
    own = own_y[...]
    own32 = own.astype(F32)
    own_half = 0.5 * jnp.sum(own32 * own32, axis=0, keepdims=True)
    ones = jnp.ones((16, chunk), BF16)
    pulled = jnp.zeros((feat + 16, rows), F32)
    for start in range(0, rows, chunk):
        part_y = vis_y[:, start : start + chunk]
        turned = part_y.astype(F32).T
        vis_half = 0.5 * jnp.sum(turned * turned, axis=1, keepdims=True)
        cross = jnp.dot(turned.astype(BF16), own, preferred_element_type=F32)
        coupling = lax.dot_general(
            vis_pair[:, start : start + chunk],
            crossed,
            (((0,), (0,)), ((), ())),
            preferred_element_type=F32,
        )
        weight = (coupling * jnp.exp(cross - (own_half + vis_half))).astype(BF16)
        pulled += jnp.dot(
            jnp.concatenate([part_y, ones], axis=0), weight, preferred_element_type=F32
        )
    after[...] = before[...] + (pulled[:feat] - own32 * pulled[feat : feat + 1])


def in_vmem(array):
    return pltpu.with_memory_space_constraint(array, pltpu.VMEM)


def couple(own_y, own_pair, vis_y, vis_pair, drift):
    rows = own_y.shape[1]
    chunk = 256 if rows % 256 == 0 else rows
    return pl.pallas_call(
        lambda *refs: couple_kernel(chunk, *refs),
        out_shape=pltpu.VMEM(drift.shape, F32),
        in_specs=[pl.BlockSpec(memory_space=pltpu.VMEM)] * 5,
        out_specs=pl.BlockSpec(memory_space=pltpu.VMEM),
        compiler_params=pltpu.CompilerParams(vmem_limit_bytes=16 << 20),
        name="couple",
    )(*map(in_vmem, (own_y, own_pair, vis_y, vis_pair, drift)))


def place_kernel(where, table, *refs):
    w_in, b_in, w_out, wide, sems = refs[-5:]
    rows, depth = w_in.shape[0] // 2, w_out.shape[0] // 2
    cols = table.shape[2]
    copies = []
    for index in range(table.shape[0]):
        chip, half = divmod(index, 2)
        wide[index] = table[index].astype(F32)
        side = where[0] ^ half
        column = pl.ds(pl.multiple_of((2 * (where[1] ^ chip) + where[2]) * cols, cols), cols)
        sources = [wide.at[index, :rows], wide.at[index, rows : rows + depth]]
        targets = [
            w_in.at[pl.ds(pl.multiple_of(side * rows, rows), rows), column],
            w_out.at[pl.ds(pl.multiple_of(side * depth, depth), depth), column],
        ]
        if half == 0:
            sources.append(wide.at[index, rows + depth : rows + depth + 1])
            targets.append(b_in.at[:, column])
        for source, target in zip(sources, targets):
            copy = pltpu.make_async_copy(source, target, sems.at[len(copies)])
            copy.start()
            copies.append(copy)
    for copy in copies:
        copy.wait()


def place(table, where, din, feat, hid, earlier):
    count, height, cols = table.shape
    shapes = (
        jax.ShapeDtypeStruct((din, hid), F32),
        jax.ShapeDtypeStruct((1, hid), F32),
        jax.ShapeDtypeStruct((feat, hid), F32),
    )
    return pl.pallas_call(
        place_kernel,
        out_shape=shapes,
        in_specs=[pl.BlockSpec(memory_space=pltpu.SMEM), pl.BlockSpec(memory_space=pltpu.VMEM)]
        + [pl.BlockSpec(memory_space=pl.ANY) for _ in earlier],
        out_specs=[pl.BlockSpec(memory_space=pl.ANY)] * 3,
        scratch_shapes=[
            pltpu.VMEM((count, height, cols), F32),
            pltpu.SemaphoreType.DMA((3 * count,)),
        ],
        input_output_aliases={2 + i: i for i in range(len(earlier))},
        compiler_params=pltpu.CompilerParams(vmem_limit_bytes=16 << 20),
        name="place",
    )(where, in_vmem(table), *earlier)


def on_device(points, w_in, b_in, w_out, inv_scale, solves, probes):
    feat = w_out.shape[1]
    reps = lax.axis_size("rep")
    blocks = lax.axis_size("blk")
    rep_index = lax.axis_index("rep")
    blk_index = lax.axis_index("blk")
    rows, din = points.shape
    hid = w_in.shape[1]
    npts = rows * blocks
    quarter = rows // reps
    cols = hid // reps

    pair = join(probes, solves)
    hidden = jnp.tanh(jnp.dot(points, w_in, preferred_element_type=F32) + b_in).astype(BF16)
    pre = lax.dot_general(w_out, hidden, (((0,), (1,)), ((), ())), preferred_element_type=F32)
    scaled = (pre * inv_scale[:, None]).astype(BF16)
    steps = range(blocks // reps)
    masks = [[visit_mask(step, r, reps) for r in range(reps)] for step in steps]
    near, far = masks[0], masks[1:]
    pairs = [fetch(pair, far[0], blocks, reps)]
    pairs += [fetch(pair, mask, blocks, reps) for mask in far[1:]]
    scaleds = [fetch(scaled, far[0], blocks, reps)]
    scaleds += [fetch(scaled, mask, blocks, reps) for mask in far[1:]]
    near_scaled = fetch(scaled, near, blocks, reps)
    near_pair, scaled = lax.optimization_barrier((pair, scaled))
    near_pair = fetch(near_pair, near, blocks, reps)
    drift = jnp.zeros((feat, rows), F32)
    drift = couple(scaled, pair, near_scaled, near_pair, drift)
    for vis_y, vis_pair in zip(scaleds, pairs):
        drift = couple(scaled, pair, vis_y, vis_pair, drift)

    drift = drift + swap(drift, (0, 0), 1, blocks, reps)
    for bit in range(1, bits_of(reps)):
        sent = drift.astype(BF16)
        got = swap(sent, (0, 0), 1 << bit, blocks, reps)
        drift = sent.astype(F32) + got.astype(F32)
    full_grad = drift * inv_scale[:, None]
    feat_grad = lax.dynamic_slice_in_dim(full_grad, rep_index * quarter, quarter, 1)
    grad_b16 = full_grad.astype(BF16)

    first = rep_index * cols
    own_hidden = lax.dynamic_slice_in_dim(hidden, first, cols, 1)
    own_w_out = lax.dynamic_slice_in_dim(w_out, first, cols, 0)
    back = lax.dot_general(
        grad_b16, own_w_out, (((0,), (1,)), ((), ())), preferred_element_type=F32
    )
    hid32 = own_hidden.astype(F32)
    pre_grad = back * (1.0 - hid32 * hid32)
    norm = 1.0 / math.sqrt(npts)
    term_w_in = lax.dot_general(
        points, pre_grad.astype(BF16), (((0,), (0,)), ((), ())), preferred_element_type=F32
    )
    term_b_in = jnp.sum(pre_grad, axis=0)
    term_w_out = lax.dot_general(
        grad_b16, own_hidden, (((1,), (0,)), ((), ())), preferred_element_type=F32
    )
    bias = jnp.broadcast_to(term_b_in[None, None], (2, 16, cols))
    halves = jnp.concatenate(
        [term_w_in.reshape(2, din // 2, cols), term_w_out.reshape(2, feat // 2, cols), bias], axis=1
    )
    halves = (halves * norm).astype(BF16)

    same = (0, 0)
    side = blk_index & 1
    core = rep_index & 1
    kept = lax.dynamic_index_in_dim(halves, side, 0, keepdims=False)
    sent = lax.dynamic_index_in_dim(halves, 1 - side, 0, keepdims=False)
    got = swap(sent, (1, 1), 0, blocks, reps)
    part = (kept.astype(F32) + got.astype(F32)).astype(BF16)
    for bit in range(1, bits_of(blocks)):
        distance = (2 << bit) - 2
        got = swap(part, (distance, distance), 0, blocks, reps)
        part = (part.astype(F32) + got.astype(F32)).astype(BF16)

    pieces = [part]
    for index in range(1, reps):
        chip, half = divmod(index, 2)
        pieces.append(swap(part, (half, half), chip << 1, blocks, reps))
    near = jnp.stack(pieces)
    other = swap(near, same, 1, blocks, reps)
    chip = rep_index >> 1
    outs = place(near, jnp.stack([side, chip, core]), din, feat, hid, ())
    outs = place(other, jnp.stack([side, chip, 1 - core]), din, feat, hid, outs)
    grad_w_in, grad_b_in, grad_w_out = outs
    grad_w_out = grad_w_out.T
    grad_b_in = grad_b_in.reshape(hid)
    return (feat_grad, grad_w_in, grad_b_in, grad_w_out)


def solution(mesh):
    in_specs = (P("blk", None), P(), P(), P(), P(), P(None, "blk"), P(None, "blk"))
    out_specs = (P(None, ("blk", "rep")), P(), P(), P())

    return jax.shard_map(
        on_device, mesh=mesh, in_specs=in_specs, out_specs=out_specs, check_vma=False
    )
```

```python
import math

import jax
import jax.numpy as jnp
from jax import lax
from jax.experimental import pallas as pl
from jax.experimental.pallas import tpu as pltpu
from jax.sharding import PartitionSpec as P


AXES = ("blk", "rep")
BF16 = jnp.bfloat16
F32 = jnp.float32


def bits_of(count):
    return count.bit_length() - 1


def visit_mask(step, rep, reps):
    width = bits_of(reps)
    core = rep & 1
    near = (core << (width - 1)) | (rep >> 1)
    if width > 1:
        near ^= core ^ (step & 1)
    return step * reps + near


def fetch(array, masks, blocks, reps):
    route = [((b ^ masks[r]) * reps + r, b * reps + r) for b in range(blocks) for r in range(reps)]
    return lax.ppermute(array, AXES, route)


def swap(array, blk_masks, rep_mask, blocks, reps):
    route = [
        (b * reps + r, (b ^ blk_masks[r & 1]) * reps + (r ^ rep_mask))
        for b in range(blocks)
        for r in range(reps)
    ]
    return lax.ppermute(array, AXES, route)


def join_kernel(first, second, joined, sems):
    count = first.shape[0]
    copies = [
        pltpu.make_async_copy(first, joined.at[:count], sems.at[0]),
        pltpu.make_async_copy(second, joined.at[count:], sems.at[1]),
    ]
    for copy in copies:
        copy.start()
    for copy in copies:
        copy.wait()


def join(first, second):
    count, rows = first.shape
    return pl.pallas_call(
        join_kernel,
        out_shape=pltpu.VMEM((2 * count, rows), first.dtype),
        in_specs=[pl.BlockSpec(memory_space=pl.ANY)] * 2,
        out_specs=pl.BlockSpec(memory_space=pltpu.VMEM),
        scratch_shapes=[pltpu.SemaphoreType.DMA((2,))],
        name="join",
    )(first, second)


def couple_kernel(chunk, own_y, own_pair, vis_y, vis_pair, before, after):
    feat, rows = own_y.shape
    count = own_pair.shape[0] // 2
    crossed = jnp.concatenate([own_pair[count:], own_pair[:count]], axis=0)
    own = own_y[...]
    own32 = own.astype(F32)
    own_half = 0.5 * jnp.sum(own32 * own32, axis=0, keepdims=True)
    ones = jnp.ones((16, chunk), BF16)
    pulled = jnp.zeros((feat + 16, rows), F32)
    for start in range(0, rows, chunk):
        part_y = vis_y[:, start : start + chunk]
        turned = part_y.astype(F32).T
        vis_half = 0.5 * jnp.sum(turned * turned, axis=1, keepdims=True)
        cross = jnp.dot(turned.astype(BF16), own, preferred_element_type=F32)
        coupling = lax.dot_general(
            vis_pair[:, start : start + chunk],
            crossed,
            (((0,), (0,)), ((), ())),
            preferred_element_type=F32,
        )
        weight = (coupling * jnp.exp(cross - (own_half + vis_half))).astype(BF16)
        pulled += jnp.dot(
            jnp.concatenate([part_y, ones], axis=0), weight, preferred_element_type=F32
        )
    after[...] = before[...] + (pulled[:feat] - own32 * pulled[feat : feat + 1])


def in_vmem(array):
    return pltpu.with_memory_space_constraint(array, pltpu.VMEM)


def couple(own_y, own_pair, vis_y, vis_pair, drift):
    rows = own_y.shape[1]
    chunk = 256 if rows % 256 == 0 else rows
    return pl.pallas_call(
        lambda *refs: couple_kernel(chunk, *refs),
        out_shape=pltpu.VMEM(drift.shape, F32),
        in_specs=[pl.BlockSpec(memory_space=pltpu.VMEM)] * 5,
        out_specs=pl.BlockSpec(memory_space=pltpu.VMEM),
        compiler_params=pltpu.CompilerParams(vmem_limit_bytes=16 << 20),
        name="couple",
    )(*map(in_vmem, (own_y, own_pair, vis_y, vis_pair, drift)))


def place_kernel(labels, *refs):
    tables, (w_in, b_in, w_out, wide, sems) = refs[: len(labels)], refs[-5:]
    rows, depth = w_in.shape[0] // 2, w_out.shape[0] // 2
    cols = tables[0].shape[2]
    own_side = lax.axis_index("blk") & 1
    own_chip = lax.axis_index("rep") >> 1
    own_core = lax.axis_index("rep") & 1
    copies = []
    count = 0
    for table, its_labels in zip(tables, labels):
        for index, (half, chip, core) in enumerate(its_labels):
            wide[count] = table[index].astype(F32)
            side = own_side ^ half
            column = 2 * (own_chip ^ chip) + (own_core ^ core)
            column = pl.ds(pl.multiple_of(column * cols, cols), cols)
            sources = [wide.at[count, :rows], wide.at[count, rows : rows + depth]]
            targets = [
                w_in.at[pl.ds(pl.multiple_of(side * rows, rows), rows), column],
                w_out.at[pl.ds(pl.multiple_of(side * depth, depth), depth), column],
            ]
            if half == 0:
                sources.append(wide.at[count, rows + depth : rows + depth + 1])
                targets.append(b_in.at[:, column])
            for source, target in zip(sources, targets):
                copy = pltpu.make_async_copy(source, target, sems.at[len(copies)])
                copy.start()
                copies.append(copy)
            count += 1
    for copy in copies:
        copy.wait()


def place(tables, labels, din, feat, hid, earlier):
    height, cols = tables[0].shape[1:]
    count = sum(len(its_labels) for its_labels in labels)
    shapes = (
        jax.ShapeDtypeStruct((din, hid), F32),
        jax.ShapeDtypeStruct((1, hid), F32),
        jax.ShapeDtypeStruct((feat, hid), F32),
    )
    return pl.pallas_call(
        lambda *refs: place_kernel(labels, *refs),
        out_shape=shapes,
        in_specs=[pl.BlockSpec(memory_space=pltpu.VMEM) for _ in tables]
        + [pl.BlockSpec(memory_space=pl.ANY) for _ in earlier],
        out_specs=[pl.BlockSpec(memory_space=pl.ANY)] * 3,
        scratch_shapes=[
            pltpu.VMEM((count, height, cols), F32),
            pltpu.SemaphoreType.DMA((3 * count,)),
        ],
        input_output_aliases={len(tables) + i: i for i in range(len(earlier))},
        compiler_params=pltpu.CompilerParams(vmem_limit_bytes=16 << 20),
        name="place",
    )(*map(in_vmem, tables), *earlier)


def on_device(points, w_in, b_in, w_out, inv_scale, solves, probes):
    feat = w_out.shape[1]
    reps = lax.axis_size("rep")
    blocks = lax.axis_size("blk")
    rep_index = lax.axis_index("rep")
    blk_index = lax.axis_index("blk")
    rows, din = points.shape
    hid = w_in.shape[1]
    npts = rows * blocks
    quarter = rows // reps
    cols = hid // reps

    pair = join(probes, solves)
    hidden = jnp.tanh(jnp.dot(points, w_in, preferred_element_type=F32) + b_in).astype(BF16)
    pre = lax.dot_general(w_out, hidden, (((0,), (1,)), ((), ())), preferred_element_type=F32)
    scaled = (pre * inv_scale[:, None]).astype(BF16)
    steps = range(blocks // reps)
    masks = [[visit_mask(step, r, reps) for r in range(reps)] for step in steps]
    near, far = masks[0], masks[1:]
    pairs = [fetch(pair, far[0], blocks, reps)]
    pairs += [fetch(pair, mask, blocks, reps) for mask in far[1:]]
    near_pair = fetch(pair, near, blocks, reps)
    scaleds = [fetch(scaled, far[0], blocks, reps)]
    scaleds += [fetch(scaled, mask, blocks, reps) for mask in far[1:]]
    near_scaled = fetch(scaled, near, blocks, reps)
    drift = jnp.zeros((feat, rows), F32)
    drift = couple(scaled, pair, near_scaled, near_pair, drift)
    for vis_y, vis_pair in zip(scaleds, pairs):
        drift = couple(scaled, pair, vis_y, vis_pair, drift)

    drift = drift + swap(drift, (0, 0), 1, blocks, reps)
    for bit in range(1, bits_of(reps)):
        sent = drift.astype(BF16)
        got = swap(sent, (0, 0), 1 << bit, blocks, reps)
        drift = sent.astype(F32) + got.astype(F32)
    full_grad = drift * inv_scale[:, None]
    feat_grad = lax.dynamic_slice_in_dim(full_grad, rep_index * quarter, quarter, 1)
    grad_b16 = full_grad.astype(BF16)

    first = rep_index * cols
    own_hidden = lax.dynamic_slice_in_dim(hidden, first, cols, 1)
    own_w_out = lax.dynamic_slice_in_dim(w_out, first, cols, 0)
    back = lax.dot_general(
        grad_b16, own_w_out, (((0,), (1,)), ((), ())), preferred_element_type=F32
    )
    hid32 = own_hidden.astype(F32)
    pre_grad = back * (1.0 - hid32 * hid32)
    norm = 1.0 / math.sqrt(npts)
    term_w_in = lax.dot_general(
        points, pre_grad.astype(BF16), (((0,), (0,)), ((), ())), preferred_element_type=F32
    )
    term_b_in = jnp.sum(pre_grad, axis=0)
    term_w_out = lax.dot_general(
        grad_b16, own_hidden, (((1,), (0,)), ((), ())), preferred_element_type=F32
    )
    bias = jnp.broadcast_to(term_b_in[None, None], (2, 16, cols))
    halves = jnp.concatenate(
        [term_w_in.reshape(2, din // 2, cols), term_w_out.reshape(2, feat // 2, cols), bias], axis=1
    )
    halves = (halves * norm).astype(BF16)

    same = (0, 0)
    side = blk_index & 1
    kept = lax.dynamic_index_in_dim(halves, side, 0, keepdims=False)
    sent = lax.dynamic_index_in_dim(halves, 1 - side, 0, keepdims=False)
    got = swap(sent, (1, 1), 0, blocks, reps)
    part = (kept.astype(F32) + got.astype(F32)).astype(BF16)
    for bit in range(1, bits_of(blocks)):
        distance = (2 << bit) - 2
        got = swap(part, (distance, distance), 0, blocks, reps)
        part = (part.astype(F32) + got.astype(F32)).astype(BF16)

    pieces = [part]
    origins = [(0, 0)]
    for index in range(1, reps):
        chip, half = divmod(index, 2)
        pieces.append(swap(part, (half, half), chip << 1, blocks, reps))
        origins.append((half, chip))
    early, late = jnp.stack(pieces[:2]), jnp.stack(pieces[2:])
    early_labels, late_labels = (
        [[(half, chip, core) for half, chip in group] for core in range(2)]
        for group in (origins[:2], origins[2:])
    )
    sizes = (din, feat, hid)
    early_other = swap(early, same, 1, blocks, reps)
    outs = place([early, early_other], early_labels, *sizes, ())
    late_other = swap(late, same, 1, blocks, reps)
    outs = place([late], late_labels[:1], *sizes, outs)
    outs = place([late_other], late_labels[1:], *sizes, outs)
    grad_w_in, grad_b_in, grad_w_out = outs
    grad_w_out = grad_w_out.T
    grad_b_in = grad_b_in.reshape(hid)
    return (feat_grad, grad_w_in, grad_b_in, grad_w_out)


def solution(mesh):
    in_specs = (P("blk", None), P(), P(), P(), P(), P(None, "blk"), P(None, "blk"))
    out_specs = (P(None, ("blk", "rep")), P(), P(), P())

    return jax.shard_map(
        on_device, mesh=mesh, in_specs=in_specs, out_specs=out_specs, check_vma=False
    )
```

```python
import math

import jax
import jax.numpy as jnp
from jax import lax
from jax.experimental import pallas as pl
from jax.experimental.pallas import tpu as pltpu
from jax.sharding import PartitionSpec as P


AXES = ("blk", "rep")
BF16 = jnp.bfloat16
F32 = jnp.float32


def bits_of(count):
    return count.bit_length() - 1


def visit_mask(step, rep, reps):
    width = bits_of(reps)
    core = rep & 1
    near = (core << (width - 1)) | (rep >> 1)
    if width > 1:
        near ^= core ^ (step & 1)
    return step * reps + near


def fetch(array, masks, blocks, reps):
    route = [((b ^ masks[r]) * reps + r, b * reps + r) for b in range(blocks) for r in range(reps)]
    return lax.ppermute(array, AXES, route)


def swap(array, blk_masks, rep_mask, blocks, reps):
    route = [
        (b * reps + r, (b ^ blk_masks[r & 1]) * reps + (r ^ rep_mask))
        for b in range(blocks)
        for r in range(reps)
    ]
    return lax.ppermute(array, AXES, route)


def join_kernel(first, second, joined, sems):
    count = first.shape[0]
    copies = [
        pltpu.make_async_copy(first, joined.at[:count], sems.at[0]),
        pltpu.make_async_copy(second, joined.at[count:], sems.at[1]),
    ]
    for copy in copies:
        copy.start()
    for copy in copies:
        copy.wait()


def join(first, second):
    count, rows = first.shape
    return pl.pallas_call(
        join_kernel,
        out_shape=pltpu.VMEM((2 * count, rows), first.dtype),
        in_specs=[pl.BlockSpec(memory_space=pl.ANY)] * 2,
        out_specs=pl.BlockSpec(memory_space=pltpu.VMEM),
        scratch_shapes=[pltpu.SemaphoreType.DMA((2,))],
        name="join",
    )(first, second)


def exponent_rows(vectors, first):
    wide = vectors.astype(F32)
    left = -0.5 * jnp.sum(wide * wide, axis=0, keepdims=True)
    parts = []
    for _ in range(3):
        part = left.astype(BF16).astype(F32)
        parts.append(part)
        left = left - part
    ones = [jnp.ones_like(left)] * 3
    rows = parts + ones if first else ones + parts
    rows.append(jnp.zeros((10, vectors.shape[1]), F32))
    return jnp.concatenate([vectors, jnp.concatenate(rows, axis=0).astype(BF16)], axis=0)


def couple_kernel(chunk, own_y, own_pair, vis_y, vis_pair, before, after):
    feat, rows = own_y.shape
    count = own_pair.shape[0] // 2
    crossed = jnp.concatenate([own_pair[count:], own_pair[:count]], axis=0)
    own = own_y[...]
    own_rows = exponent_rows(own, True)
    ones = jnp.ones((16, chunk), BF16)
    pulled = jnp.zeros((feat + 16, rows), F32)
    over_rows = (((0,), (0,)), ((), ()))
    for start in range(0, rows, chunk):
        part_y = vis_y[:, start : start + chunk]
        coupling = lax.dot_general(
            vis_pair[:, start : start + chunk], crossed, over_rows, preferred_element_type=F32
        )
        exponent = lax.dot_general(
            exponent_rows(part_y, False), own_rows, over_rows, preferred_element_type=F32
        )
        weight = (coupling * jnp.exp(exponent)).astype(BF16)
        pulled += jnp.dot(
            jnp.concatenate([part_y, ones], axis=0), weight, preferred_element_type=F32
        )
    after[...] = before[...] + (pulled[:feat] - own.astype(F32) * pulled[feat : feat + 1])


def in_vmem(array):
    return pltpu.with_memory_space_constraint(array, pltpu.VMEM)


def couple(own_y, own_pair, vis_y, vis_pair, drift):
    rows = own_y.shape[1]
    chunk = 256 if rows > 1024 and rows % 256 == 0 else rows
    return pl.pallas_call(
        lambda *refs: couple_kernel(chunk, *refs),
        out_shape=pltpu.VMEM(drift.shape, F32),
        in_specs=[pl.BlockSpec(memory_space=pltpu.VMEM)] * 5,
        out_specs=pl.BlockSpec(memory_space=pltpu.VMEM),
        compiler_params=pltpu.CompilerParams(vmem_limit_bytes=24 << 20),
        name="couple",
    )(*map(in_vmem, (own_y, own_pair, vis_y, vis_pair, drift)))


def place_kernel(labels, *refs):
    tables, (w_in, b_in, w_out, wide, sems) = refs[: len(labels)], refs[-5:]
    rows, depth = w_in.shape[0] // 2, w_out.shape[0] // 2
    cols = tables[0].shape[2]
    own_side = lax.axis_index("blk") & 1
    own_chip = lax.axis_index("rep") >> 1
    own_core = lax.axis_index("rep") & 1
    copies = []
    count = 0
    for table, its_labels in zip(tables, labels):
        for index, (half, chip, core) in enumerate(its_labels):
            wide[count] = table[index].astype(F32)
            side = own_side ^ half
            column = 2 * (own_chip ^ chip) + (own_core ^ core)
            column = pl.ds(pl.multiple_of(column * cols, cols), cols)
            sources = [wide.at[count, :rows], wide.at[count, rows : rows + depth]]
            targets = [
                w_in.at[pl.ds(pl.multiple_of(side * rows, rows), rows), column],
                w_out.at[pl.ds(pl.multiple_of(side * depth, depth), depth), column],
            ]
            if half == 0:
                sources.append(wide.at[count, rows + depth : rows + depth + 1])
                targets.append(b_in.at[:, column])
            for source, target in zip(sources, targets):
                copy = pltpu.make_async_copy(source, target, sems.at[len(copies)])
                copy.start()
                copies.append(copy)
            count += 1
    for copy in copies:
        copy.wait()


def place(tables, labels, din, feat, hid, earlier):
    height, cols = tables[0].shape[1:]
    count = sum(len(its_labels) for its_labels in labels)
    shapes = (
        jax.ShapeDtypeStruct((din, hid), F32),
        jax.ShapeDtypeStruct((1, hid), F32),
        jax.ShapeDtypeStruct((feat, hid), F32),
    )
    return pl.pallas_call(
        lambda *refs: place_kernel(labels, *refs),
        out_shape=shapes,
        in_specs=[pl.BlockSpec(memory_space=pltpu.VMEM) for _ in tables]
        + [pl.BlockSpec(memory_space=pl.ANY) for _ in earlier],
        out_specs=[pl.BlockSpec(memory_space=pl.ANY)] * 3,
        scratch_shapes=[
            pltpu.VMEM((count, height, cols), F32),
            pltpu.SemaphoreType.DMA((3 * count,)),
        ],
        input_output_aliases={len(tables) + i: i for i in range(len(earlier))},
        compiler_params=pltpu.CompilerParams(vmem_limit_bytes=16 << 20),
        name="place",
    )(*map(in_vmem, tables), *earlier)


def on_device(points, w_in, b_in, w_out, inv_scale, solves, probes):
    feat = w_out.shape[1]
    reps = lax.axis_size("rep")
    blocks = lax.axis_size("blk")
    rep_index = lax.axis_index("rep")
    blk_index = lax.axis_index("blk")
    rows, din = points.shape
    hid = w_in.shape[1]
    npts = rows * blocks
    quarter = rows // reps
    cols = hid // reps

    pair = join(probes, solves)
    hidden = jnp.tanh(jnp.dot(points, w_in, preferred_element_type=F32) + b_in).astype(BF16)
    pre = lax.dot_general(w_out, hidden, (((0,), (1,)), ((), ())), preferred_element_type=F32)
    scaled = (pre * inv_scale[:, None]).astype(BF16)
    steps = range(blocks // reps)
    masks = [[visit_mask(step, r, reps) for r in range(reps)] for step in steps]
    near, far = masks[0], masks[1:]
    pairs = [fetch(pair, far[0], blocks, reps)]
    pairs += [fetch(pair, mask, blocks, reps) for mask in far[1:]]
    near_pair = fetch(pair, near, blocks, reps)
    scaleds = [fetch(scaled, far[0], blocks, reps)]
    scaleds += [fetch(scaled, mask, blocks, reps) for mask in far[1:]]
    near_scaled = fetch(scaled, near, blocks, reps)
    drift = jnp.zeros((feat, rows), F32)
    drift = couple(scaled, pair, near_scaled, near_pair, drift)
    for vis_y, vis_pair in zip(scaleds, pairs):
        drift = couple(scaled, pair, vis_y, vis_pair, drift)

    drift = drift + swap(drift, (0, 0), 1, blocks, reps)
    for bit in range(1, bits_of(reps)):
        sent = drift.astype(BF16)
        got = swap(sent, (0, 0), 1 << bit, blocks, reps)
        drift = sent.astype(F32) + got.astype(F32)
    full_grad = drift * inv_scale[:, None]
    feat_grad = lax.dynamic_slice_in_dim(full_grad, rep_index * quarter, quarter, 1)
    grad_b16 = full_grad.astype(BF16)

    first = rep_index * cols
    own_hidden = lax.dynamic_slice_in_dim(hidden, first, cols, 1)
    own_w_out = lax.dynamic_slice_in_dim(w_out, first, cols, 0)
    back = lax.dot_general(
        grad_b16, own_w_out, (((0,), (1,)), ((), ())), preferred_element_type=F32
    )
    hid32 = own_hidden.astype(F32)
    pre_grad = back * (1.0 - hid32 * hid32)
    norm = 1.0 / math.sqrt(npts)
    term_w_in = lax.dot_general(
        points, pre_grad.astype(BF16), (((0,), (0,)), ((), ())), preferred_element_type=F32
    )
    term_b_in = jnp.sum(pre_grad, axis=0)
    term_w_out = lax.dot_general(
        grad_b16, own_hidden, (((1,), (0,)), ((), ())), preferred_element_type=F32
    )
    bias = jnp.broadcast_to(term_b_in[None, None], (2, 16, cols))
    halves = jnp.concatenate(
        [term_w_in.reshape(2, din // 2, cols), term_w_out.reshape(2, feat // 2, cols), bias], axis=1
    )
    halves = (halves * norm).astype(BF16)

    same = (0, 0)
    side = blk_index & 1
    kept = lax.dynamic_index_in_dim(halves, side, 0, keepdims=False)
    sent = lax.dynamic_index_in_dim(halves, 1 - side, 0, keepdims=False)
    got = swap(sent, (1, 1), 0, blocks, reps)
    part = (kept.astype(F32) + got.astype(F32)).astype(BF16)
    for bit in range(1, bits_of(blocks)):
        distance = (2 << bit) - 2
        got = swap(part, (distance, distance), 0, blocks, reps)
        part = (part.astype(F32) + got.astype(F32)).astype(BF16)

    pieces = [part]
    origins = [(0, 0)]
    for index in range(1, reps):
        chip, half = divmod(index, 2)
        pieces.append(swap(part, (half, half), chip << 1, blocks, reps))
        origins.append((half, chip))
    early, late = jnp.stack(pieces[:2]), jnp.stack(pieces[2:])
    early_labels, late_labels = (
        [[(half, chip, core) for half, chip in group] for core in range(2)]
        for group in (origins[:2], origins[2:])
    )
    sizes = (din, feat, hid)
    early_other = swap(early, same, 1, blocks, reps)
    outs = place([early, early_other], early_labels, *sizes, ())
    late_other = swap(late, same, 1, blocks, reps)
    outs = place([late], late_labels[:1], *sizes, outs)
    outs = place([late_other], late_labels[1:], *sizes, outs)
    grad_w_in, grad_b_in, grad_w_out = outs
    grad_w_out = grad_w_out.T
    grad_b_in = grad_b_in.reshape(hid)
    return (feat_grad, grad_w_in, grad_b_in, grad_w_out)


def solution(mesh):
    in_specs = (P("blk", None), P(), P(), P(), P(), P(None, "blk"), P(None, "blk"))
    out_specs = (P(None, ("blk", "rep")), P(), P(), P())

    return jax.shard_map(
        on_device, mesh=mesh, in_specs=in_specs, out_specs=out_specs, check_vma=False
    )
```

```python
import math

import jax
import jax.numpy as jnp
from jax import lax
from jax.experimental import pallas as pl
from jax.experimental.pallas import tpu as pltpu
from jax.sharding import PartitionSpec as P


AXES = ("blk", "rep")
BF16 = jnp.bfloat16
F32 = jnp.float32


def bits_of(count):
    return count.bit_length() - 1


def visit_mask(step, rep, reps):
    width = bits_of(reps)
    core = rep & 1
    near = (core << (width - 1)) | (rep >> 1)
    if width > 1:
        near ^= core ^ (step & 1)
    return step * reps + near


def fetch(array, masks, blocks, reps):
    route = [((b ^ masks[r]) * reps + r, b * reps + r) for b in range(blocks) for r in range(reps)]
    return lax.ppermute(array, AXES, route)


def swap(array, blk_masks, rep_mask, blocks, reps):
    route = [
        (b * reps + r, (b ^ blk_masks[r & 1]) * reps + (r ^ rep_mask))
        for b in range(blocks)
        for r in range(reps)
    ]
    return lax.ppermute(array, AXES, route)


def join_kernel(first, second, joined, sems):
    count = first.shape[0]
    copies = [
        pltpu.make_async_copy(first, joined.at[:count], sems.at[0]),
        pltpu.make_async_copy(second, joined.at[count:], sems.at[1]),
    ]
    for copy in copies:
        copy.start()
    for copy in copies:
        copy.wait()


def join(first, second):
    count, rows = first.shape
    return pl.pallas_call(
        join_kernel,
        out_shape=pltpu.VMEM((2 * count, rows), first.dtype),
        in_specs=[pl.BlockSpec(memory_space=pl.ANY)] * 2,
        out_specs=pl.BlockSpec(memory_space=pltpu.VMEM),
        scratch_shapes=[pltpu.SemaphoreType.DMA((2,))],
        name="join",
    )(first, second)


def exponent_rows(vectors, first):
    wide = vectors.astype(F32)
    left = -0.5 * jnp.sum(wide * wide, axis=0, keepdims=True)
    parts = []
    for _ in range(3):
        part = left.astype(BF16).astype(F32)
        parts.append(part)
        left = left - part
    ones = [jnp.ones_like(left)] * 3
    rows = parts + ones if first else ones + parts
    rows.append(jnp.zeros((10, vectors.shape[1]), F32))
    return jnp.concatenate([vectors, jnp.concatenate(rows, axis=0).astype(BF16)], axis=0)


def couple_kernel(chunk, own_y, own_pair, vis_y, vis_pair, before, after):
    feat, rows = own_y.shape
    count = own_pair.shape[0] // 2
    crossed = jnp.concatenate([own_pair[count:], own_pair[:count]], axis=0)
    own = own_y[...]
    own_rows = exponent_rows(own, True)
    ones = jnp.ones((16, chunk), BF16)
    pulled = jnp.zeros((feat + 16, rows), F32)
    over_rows = (((0,), (0,)), ((), ()))
    for start in range(0, rows, chunk):
        part_y = vis_y[:, start : start + chunk]
        coupling = lax.dot_general(
            vis_pair[:, start : start + chunk], crossed, over_rows, preferred_element_type=F32
        )
        exponent = lax.dot_general(
            exponent_rows(part_y, False), own_rows, over_rows, preferred_element_type=F32
        )
        weight = (coupling * jnp.exp(exponent)).astype(BF16)
        pulled += jnp.dot(
            jnp.concatenate([part_y, ones], axis=0), weight, preferred_element_type=F32
        )
    after[...] = before[...] + (pulled[:feat] - own.astype(F32) * pulled[feat : feat + 1])


def in_vmem(array):
    return pltpu.with_memory_space_constraint(array, pltpu.VMEM)


def couple(own_y, own_pair, vis_y, vis_pair, drift):
    rows = own_y.shape[1]
    chunk = 256 if rows > 1024 and rows % 256 == 0 else rows
    return pl.pallas_call(
        lambda *refs: couple_kernel(chunk, *refs),
        out_shape=pltpu.VMEM(drift.shape, F32),
        in_specs=[pl.BlockSpec(memory_space=pltpu.VMEM)] * 5,
        out_specs=pl.BlockSpec(memory_space=pltpu.VMEM),
        compiler_params=pltpu.CompilerParams(vmem_limit_bytes=24 << 20),
        name="couple",
    )(*map(in_vmem, (own_y, own_pair, vis_y, vis_pair, drift)))


def place_kernel(labels, *refs):
    tables, (w_in, b_in, w_out, wide, sems) = refs[: len(labels)], refs[-5:]
    rows, depth = w_in.shape[0] // 2, w_out.shape[0] // 2
    cols = tables[0].shape[2]
    own_side = lax.axis_index("blk") & 1
    own_chip = lax.axis_index("rep") >> 1
    own_core = lax.axis_index("rep") & 1
    copies = []
    count = 0
    for table, its_labels in zip(tables, labels):
        for index, (half, chip, core) in enumerate(its_labels):
            wide[count] = table[index].astype(F32)
            side = own_side ^ half
            column = 2 * (own_chip ^ chip) + (own_core ^ core)
            column = pl.ds(pl.multiple_of(column * cols, cols), cols)
            sources = [wide.at[count, :rows], wide.at[count, rows : rows + depth]]
            targets = [
                w_in.at[pl.ds(pl.multiple_of(side * rows, rows), rows), column],
                w_out.at[pl.ds(pl.multiple_of(side * depth, depth), depth), column],
            ]
            if half == 0:
                sources.append(wide.at[count, rows + depth : rows + depth + 1])
                targets.append(b_in.at[:, column])
            for source, target in zip(sources, targets):
                copy = pltpu.make_async_copy(source, target, sems.at[len(copies)])
                copy.start()
                copies.append(copy)
            count += 1
    for copy in copies:
        copy.wait()


def place(tables, labels, din, feat, hid, earlier):
    height, cols = tables[0].shape[1:]
    count = sum(len(its_labels) for its_labels in labels)
    shapes = (
        jax.ShapeDtypeStruct((din, hid), F32),
        jax.ShapeDtypeStruct((1, hid), F32),
        jax.ShapeDtypeStruct((feat, hid), F32),
    )
    return pl.pallas_call(
        lambda *refs: place_kernel(labels, *refs),
        out_shape=shapes,
        in_specs=[pl.BlockSpec(memory_space=pltpu.VMEM) for _ in tables]
        + [pl.BlockSpec(memory_space=pl.ANY) for _ in earlier],
        out_specs=[pl.BlockSpec(memory_space=pl.ANY)] * 3,
        scratch_shapes=[
            pltpu.VMEM((count, height, cols), F32),
            pltpu.SemaphoreType.DMA((3 * count,)),
        ],
        input_output_aliases={len(tables) + i: i for i in range(len(earlier))},
        compiler_params=pltpu.CompilerParams(vmem_limit_bytes=16 << 20),
        name="place",
    )(*map(in_vmem, tables), *earlier)


def on_device(points, w_in, b_in, w_out, inv_scale, solves, probes):
    feat = w_out.shape[1]
    reps = lax.axis_size("rep")
    blocks = lax.axis_size("blk")
    rep_index = lax.axis_index("rep")
    blk_index = lax.axis_index("blk")
    rows, din = points.shape
    hid = w_in.shape[1]
    npts = rows * blocks
    quarter = rows // reps
    cols = hid // reps

    pair = join(probes, solves)
    hidden = jnp.tanh(jnp.dot(points, w_in, preferred_element_type=F32) + b_in).astype(BF16)
    pre = lax.dot_general(w_out, hidden, (((0,), (1,)), ((), ())), preferred_element_type=F32)
    scaled = (pre * inv_scale[:, None]).astype(BF16)
    steps = range(blocks // reps)
    masks = [[visit_mask(step, r, reps) for r in range(reps)] for step in steps]
    near, far = masks[0], masks[1:]
    pairs = [fetch(pair, far[0], blocks, reps)]
    pairs += [fetch(pair, mask, blocks, reps) for mask in far[1:]]
    near_pair = fetch(pair, near, blocks, reps)
    scaleds = [fetch(scaled, far[0], blocks, reps)]
    scaleds += [fetch(scaled, mask, blocks, reps) for mask in far[1:]]
    near_scaled = fetch(scaled, near, blocks, reps)
    drift = jnp.zeros((feat, rows), F32)
    drift = couple(scaled, pair, near_scaled, near_pair, drift)
    for vis_y, vis_pair in zip(scaleds, pairs):
        drift = couple(scaled, pair, vis_y, vis_pair, drift)

    drift = drift + swap(drift, (0, 0), 1, blocks, reps)
    for bit in range(1, bits_of(reps)):
        sent = drift.astype(BF16)
        got = swap(sent, (0, 0), 1 << bit, blocks, reps)
        drift = sent.astype(F32) + got.astype(F32)
    full_grad = drift * inv_scale[:, None]
    feat_grad = lax.dynamic_slice_in_dim(full_grad, rep_index * quarter, quarter, 1)
    grad_b16 = full_grad.astype(BF16)

    first = rep_index * cols
    own_hidden = lax.dynamic_slice_in_dim(hidden, first, cols, 1)
    own_w_out = lax.dynamic_slice_in_dim(w_out, first, cols, 0)
    back = lax.dot_general(
        grad_b16, own_w_out, (((0,), (1,)), ((), ())), preferred_element_type=F32
    )
    hid32 = own_hidden.astype(F32)
    pre_grad = back * (1.0 - hid32 * hid32)
    norm = 1.0 / math.sqrt(npts)
    term_w_in = lax.dot_general(
        points, pre_grad.astype(BF16), (((0,), (0,)), ((), ())), preferred_element_type=F32
    )
    term_b_in = jnp.sum(pre_grad, axis=0)
    term_w_out = lax.dot_general(
        grad_b16, own_hidden, (((1,), (0,)), ((), ())), preferred_element_type=F32
    )
    bias = jnp.broadcast_to(term_b_in[None, None], (2, 16, cols))
    halves = jnp.concatenate(
        [term_w_in.reshape(2, din // 2, cols), term_w_out.reshape(2, feat // 2, cols), bias], axis=1
    )
    halves = (halves * norm).astype(BF16)

    same = (0, 0)
    side = blk_index & 1
    kept = lax.dynamic_index_in_dim(halves, side, 0, keepdims=False)
    sent = lax.dynamic_index_in_dim(halves, 1 - side, 0, keepdims=False)
    got = swap(sent, (1, 1), 0, blocks, reps)
    part = (kept.astype(F32) + got.astype(F32)).astype(BF16)
    for bit in range(1, bits_of(blocks)):
        distance = (2 << bit) - 2
        got = swap(part, (distance, distance), 0, blocks, reps)
        part = (part.astype(F32) + got.astype(F32)).astype(BF16)

    pieces = [part]
    origins = [(0, 0)]
    for index in range(1, reps):
        chip, half = divmod(index, 2)
        pieces.append(swap(part, (half, half), chip << 1, blocks, reps))
        origins.append((half, chip))
    sizes = (din, feat, hid)
    groups = (pieces[:1], pieces[1:-1], pieces[-1:])
    labels = [
        [[(half, chip, core) for half, chip in group] for core in range(2)]
        for group in (origins[:1], origins[1:-1], origins[-1:])
    ]
    tables = [jnp.stack(group) for group in groups]
    others = []
    for table in tables:
        others.append(swap(table, same, 1, blocks, reps))
    outs = place([tables[0], others[0]], labels[0], *sizes, ())
    outs = place(
        [tables[1], others[1], tables[2]], [*labels[1], labels[2][0]], *sizes, outs
    )
    outs = place([others[2]], labels[2][1:], *sizes, outs)
    grad_w_in, grad_b_in, grad_w_out = outs
    grad_w_out = grad_w_out.T
    grad_b_in = grad_b_in.reshape(hid)
    return (feat_grad, grad_w_in, grad_b_in, grad_w_out)


def solution(mesh):
    in_specs = (P("blk", None), P(), P(), P(), P(), P(None, "blk"), P(None, "blk"))
    out_specs = (P(None, ("blk", "rep")), P(), P(), P())

    return jax.shard_map(
        on_device, mesh=mesh, in_specs=in_specs, out_specs=out_specs, check_vma=False
    )
```

```python
import math

import jax
import jax.numpy as jnp
from jax import lax
from jax.experimental import pallas as pl
from jax.experimental.pallas import tpu as pltpu
from jax.sharding import PartitionSpec as P


AXES = ("blk", "rep")
BF16 = jnp.bfloat16
F32 = jnp.float32


def bits_of(count):
    return count.bit_length() - 1


def visit_mask(step, rep, reps):
    width = bits_of(reps)
    core = rep & 1
    near = (core << (width - 1)) | (rep >> 1)
    if width > 1:
        near ^= core ^ (step & 1)
    return step * reps + near


def fetch(array, masks, blocks, reps):
    route = [((b ^ masks[r]) * reps + r, b * reps + r) for b in range(blocks) for r in range(reps)]
    return lax.ppermute(array, AXES, route)


def swap(array, blk_masks, rep_mask, blocks, reps):
    route = [
        (b * reps + r, (b ^ blk_masks[r & 1]) * reps + (r ^ rep_mask))
        for b in range(blocks)
        for r in range(reps)
    ]
    return lax.ppermute(array, AXES, route)


def join_kernel(first, second, joined, sems):
    count = first.shape[0]
    copies = [
        pltpu.make_async_copy(first, joined.at[:count], sems.at[0]),
        pltpu.make_async_copy(second, joined.at[count:], sems.at[1]),
    ]
    for copy in copies:
        copy.start()
    for copy in copies:
        copy.wait()


def join(first, second):
    count, rows = first.shape
    return pl.pallas_call(
        join_kernel,
        out_shape=pltpu.VMEM((2 * count, rows), first.dtype),
        in_specs=[pl.BlockSpec(memory_space=pl.ANY)] * 2,
        out_specs=pl.BlockSpec(memory_space=pltpu.VMEM),
        scratch_shapes=[pltpu.SemaphoreType.DMA((2,))],
        name="join",
    )(first, second)


def exponent_rows(vectors, first):
    wide = vectors.astype(F32)
    left = -0.5 * jnp.sum(wide * wide, axis=0, keepdims=True)
    parts = []
    for _ in range(3):
        part = left.astype(BF16).astype(F32)
        parts.append(part)
        left = left - part
    ones = [jnp.ones_like(left)] * 3
    rows = parts + ones if first else ones + parts
    rows.append(jnp.zeros((10, vectors.shape[1]), F32))
    return jnp.concatenate([vectors, jnp.concatenate(rows, axis=0).astype(BF16)], axis=0)


def couple_kernel(chunk, own_y, own_pair, vis_y, vis_pair, before, after):
    feat, rows = own_y.shape
    count = own_pair.shape[0] // 2
    crossed = jnp.concatenate([own_pair[count:], own_pair[:count]], axis=0)
    own = own_y[...]
    own_rows = exponent_rows(own, True)
    ones = jnp.ones((16, chunk), BF16)
    pulled = jnp.zeros((feat + 16, rows), F32)
    over_rows = (((0,), (0,)), ((), ()))
    for start in range(0, rows, chunk):
        part_y = vis_y[:, start : start + chunk]
        coupling = lax.dot_general(
            vis_pair[:, start : start + chunk], crossed, over_rows, preferred_element_type=F32
        )
        exponent = lax.dot_general(
            exponent_rows(part_y, False), own_rows, over_rows, preferred_element_type=F32
        )
        weight = (coupling * jnp.exp(exponent)).astype(BF16)
        pulled += jnp.dot(
            jnp.concatenate([part_y, ones], axis=0), weight, preferred_element_type=F32
        )
    after[...] = before[...] + (pulled[:feat] - own.astype(F32) * pulled[feat : feat + 1])


def in_vmem(array):
    return pltpu.with_memory_space_constraint(array, pltpu.VMEM)


def couple(own_y, own_pair, vis_y, vis_pair, drift):
    rows = own_y.shape[1]
    chunk = 256 if rows > 1024 and rows % 256 == 0 else rows
    return pl.pallas_call(
        lambda *refs: couple_kernel(chunk, *refs),
        out_shape=pltpu.VMEM(drift.shape, F32),
        in_specs=[pl.BlockSpec(memory_space=pltpu.VMEM)] * 5,
        out_specs=pl.BlockSpec(memory_space=pltpu.VMEM),
        compiler_params=pltpu.CompilerParams(vmem_limit_bytes=24 << 20),
        name="couple",
    )(*map(in_vmem, (own_y, own_pair, vis_y, vis_pair, drift)))


def place_kernel(labels, *refs):
    tables, (w_in, b_in, w_out, wide, sems) = refs[: len(labels)], refs[-5:]
    rows, depth = w_in.shape[0] // 2, w_out.shape[0] // 2
    cols = tables[0].shape[2]
    own_side = lax.axis_index("blk") & 1
    own_chip = lax.axis_index("rep") >> 1
    own_core = lax.axis_index("rep") & 1
    copies = []
    count = 0
    for table, its_labels in zip(tables, labels):
        for index, (half, chip, core) in enumerate(its_labels):
            wide[count] = table[index].astype(F32)
            side = own_side ^ half
            column = 2 * (own_chip ^ chip) + (own_core ^ core)
            column = pl.ds(pl.multiple_of(column * cols, cols), cols)
            sources = [wide.at[count, :rows], wide.at[count, rows : rows + depth]]
            targets = [
                w_in.at[pl.ds(pl.multiple_of(side * rows, rows), rows), column],
                w_out.at[pl.ds(pl.multiple_of(side * depth, depth), depth), column],
            ]
            if half == 0:
                sources.append(wide.at[count, rows + depth : rows + depth + 1])
                targets.append(b_in.at[:, column])
            for source, target in zip(sources, targets):
                copy = pltpu.make_async_copy(source, target, sems.at[len(copies)])
                copy.start()
                copies.append(copy)
            count += 1
    for copy in copies:
        copy.wait()


def place(tables, labels, din, feat, hid, earlier):
    height, cols = tables[0].shape[1:]
    count = sum(len(its_labels) for its_labels in labels)
    shapes = (
        jax.ShapeDtypeStruct((din, hid), F32),
        jax.ShapeDtypeStruct((1, hid), F32),
        jax.ShapeDtypeStruct((feat, hid), F32),
    )
    return pl.pallas_call(
        lambda *refs: place_kernel(labels, *refs),
        out_shape=shapes,
        in_specs=[pl.BlockSpec(memory_space=pltpu.VMEM) for _ in tables]
        + [pl.BlockSpec(memory_space=pl.ANY) for _ in earlier],
        out_specs=[pl.BlockSpec(memory_space=pl.ANY)] * 3,
        scratch_shapes=[
            pltpu.VMEM((count, height, cols), F32),
            pltpu.SemaphoreType.DMA((3 * count,)),
        ],
        input_output_aliases={len(tables) + i: i for i in range(len(earlier))},
        compiler_params=pltpu.CompilerParams(vmem_limit_bytes=16 << 20),
        name="place",
    )(*map(in_vmem, tables), *earlier)


def on_device(points, w_in, b_in, w_out, inv_scale, solves, probes):
    feat = w_out.shape[1]
    reps = lax.axis_size("rep")
    blocks = lax.axis_size("blk")
    rep_index = lax.axis_index("rep")
    blk_index = lax.axis_index("blk")
    rows, din = points.shape
    hid = w_in.shape[1]
    npts = rows * blocks
    quarter = rows // reps
    cols = hid // reps

    pair = join(probes, solves)
    hidden = jnp.tanh(jnp.dot(points, w_in, preferred_element_type=F32) + b_in).astype(BF16)
    pre = lax.dot_general(w_out, hidden, (((0,), (1,)), ((), ())), preferred_element_type=F32)
    scaled = (pre * inv_scale[:, None]).astype(BF16)
    steps = range(blocks // reps)
    masks = [[visit_mask(step, r, reps) for r in range(reps)] for step in steps]
    near, far = masks[0], masks[1:]
    pairs = [fetch(pair, far[0], blocks, reps)]
    pairs += [fetch(pair, mask, blocks, reps) for mask in far[1:]]
    near_pair = fetch(pair, near, blocks, reps)
    scaleds = [fetch(scaled, far[0], blocks, reps)]
    scaleds += [fetch(scaled, mask, blocks, reps) for mask in far[1:]]
    near_scaled = fetch(scaled, near, blocks, reps)
    drift = jnp.zeros((feat, rows), F32)
    drift = couple(scaled, pair, near_scaled, near_pair, drift)
    for vis_y, vis_pair in zip(scaleds, pairs):
        drift = couple(scaled, pair, vis_y, vis_pair, drift)

    sent = drift.astype(BF16)
    drift = sent.astype(F32) + swap(sent, (0, 0), 1, blocks, reps).astype(F32)
    for bit in range(1, bits_of(reps)):
        sent = drift.astype(BF16)
        got = swap(sent, (0, 0), 1 << bit, blocks, reps)
        drift = sent.astype(F32) + got.astype(F32)
    full_grad = drift * inv_scale[:, None]
    feat_grad = lax.dynamic_slice_in_dim(full_grad, rep_index * quarter, quarter, 1)
    grad_b16 = full_grad.astype(BF16)

    first = rep_index * cols
    own_hidden = lax.dynamic_slice_in_dim(hidden, first, cols, 1)
    own_w_out = lax.dynamic_slice_in_dim(w_out, first, cols, 0)
    back = lax.dot_general(
        grad_b16, own_w_out, (((0,), (1,)), ((), ())), preferred_element_type=F32
    )
    hid32 = own_hidden.astype(F32)
    pre_grad = back * (1.0 - hid32 * hid32)
    norm = 1.0 / math.sqrt(npts)
    pre_b16 = pre_grad.astype(BF16)
    term_b_in = jnp.sum(pre_grad, axis=0)
    bias = jnp.broadcast_to(term_b_in[None], (16, cols))

    def half_of_rows(which):
        own_points = lax.dynamic_slice_in_dim(points, which * (din // 2), din // 2, 1)
        own_grad = lax.dynamic_slice_in_dim(grad_b16, which * (feat // 2), feat // 2, 0)
        term_w_in = lax.dot_general(
            own_points, pre_b16, (((0,), (0,)), ((), ())), preferred_element_type=F32
        )
        term_w_out = lax.dot_general(
            own_grad, own_hidden, (((1,), (0,)), ((), ())), preferred_element_type=F32
        )
        return (jnp.concatenate([term_w_in, term_w_out, bias], axis=0) * norm).astype(BF16)

    same = (0, 0)
    side = blk_index & 1
    given = half_of_rows(1 - side)
    got = swap(given, (1, 1), 0, blocks, reps)
    kept = half_of_rows(side)
    part = (kept.astype(F32) + got.astype(F32)).astype(BF16)
    for bit in range(1, bits_of(blocks)):
        distance = (2 << bit) - 2
        got = swap(part, (distance, distance), 0, blocks, reps)
        part = (part.astype(F32) + got.astype(F32)).astype(BF16)

    pieces = [part]
    origins = [(0, 0)]
    for index in range(1, reps):
        chip, half = divmod(index, 2)
        pieces.append(swap(part, (half, half), chip << 1, blocks, reps))
        origins.append((half, chip))
    sizes = (din, feat, hid)
    groups = (pieces[:1], pieces[1:-1], pieces[-1:])
    labels = [
        [[(half, chip, core) for half, chip in group] for core in range(2)]
        for group in (origins[:1], origins[1:-1], origins[-1:])
    ]
    tables = [jnp.stack(group) for group in groups]
    others = []
    for table in tables:
        others.append(swap(table, same, 1, blocks, reps))
    outs = place([tables[0], others[0]], labels[0], *sizes, ())
    outs = place(
        [tables[1], others[1], tables[2]], [*labels[1], labels[2][0]], *sizes, outs
    )
    outs = place([others[2]], labels[2][1:], *sizes, outs)
    grad_w_in, grad_b_in, grad_w_out = outs
    grad_w_out = grad_w_out.T
    grad_b_in = grad_b_in.reshape(hid)
    return (feat_grad, grad_w_in, grad_b_in, grad_w_out)


def solution(mesh):
    in_specs = (P("blk", None), P(), P(), P(), P(), P(None, "blk"), P(None, "blk"))
    out_specs = (P(None, ("blk", "rep")), P(), P(), P())

    return jax.shard_map(
        on_device, mesh=mesh, in_specs=in_specs, out_specs=out_specs, check_vma=False
    )
```
